128 devices in a mesh: depth: 64 (over x_lo, y, z, core), filt: 2 (over x_hi).
Axes of the slice: x: 4 (x_hi: 2, x_lo: 2; x = x_hi * 2 + x_lo), y: 4, z: 4, core: 2. Of those that a mesh axis runs over, the one named last changes fastest.
Arguments:
- volume: bfloat16 [128, 64, 1024], P('filt', 'depth'), may hold values from -6 to 6
- up_weight: bfloat16 [128, 4096], P(None, 'filt'), may hold values from -0.1875 to 0.1875
- up_bias: float32 [64], P('filt'), may hold values from -3 to 3
- first_weight: bfloat16 [27, 4096], replicated, may hold values from -0.15625 to 0.15625
- first_bias: float32 [64], replicated, may hold values from -3 to 3
- second_weight: bfloat16 [27, 4096], replicated, may hold values from -0.15625 to 0.15625
- second_bias: float32 [64], replicated, may hold values from -3 to 3
Outputs:
- decoded: bfloat16 [64, 128, 32, 128], P('filt', 'depth')
The draws below stay inside these ranges and needn't reach their ends.
All inputs are finite; a program needn't handle non-finite values.
Results may differ from the reference program's by a relative error of at most 0.0052.
Values may be sent and summed in bfloat16 or wider, within the bound.
No kernel may reach another device: no remote copies, remote signals or barrier semaphores. Data moves between devices by JAX's collectives and lax.ppermute only.
A program may use at most 64 MiB of HBM per device.

```python
import jax
import jax.numpy as jnp
from jax import lax

C_IN = 128
C_OUT = 64
IN_H = 16
IN_HW = 64
IN_DEPTH = 64


def level_of(own_key, shape, cuts, smallest, top_value):
    def one(axis_at, blocks):
        draws = jax.random.uniform(jax.random.fold_in(jax.random.fold_in(own_key, 6), axis_at), (blocks,), jnp.float32, smallest / len(cuts), top_value / len(cuts))
        return jnp.repeat(jnp.exp(draws), shape[axis_at] // blocks).reshape((-1,) + (1,) * (len(shape) - axis_at - 1))

    factor_of = one(*cuts[0])
    for cut in cuts[1:]:
        factor_of = factor_of * one(*cut)
    return factor_of


def scatter_about(key, extent, width, most, pieces=(), kind=jnp.bfloat16):
    drawn = width * jax.random.normal(key, extent, jnp.float32)
    if pieces:
        drawn = drawn * level_of(key, extent, pieces, -0.22, 0.18)
    return jnp.clip(drawn, -most, most).astype(kind)


def setup_inputs(seed: int = 0) -> dict:
    seeds = jax.random.split(jax.random.key(seed), 8)
    return {
        "volume": scatter_about(seeds[0], (C_IN, IN_DEPTH, IN_H * IN_HW), 1.0, 6.0, ((0, 2), (1, 64))),
        "up_weight": scatter_about(seeds[1], (C_IN, C_OUT * 64), (C_IN * 8) ** -0.5, 0.1875, ((1, 2),)),
        "up_bias": scatter_about(seeds[2], (C_OUT,), 0.5, 3.0, ((0, 2),), jnp.float32),
        "first_weight": scatter_about(seeds[3], (27, C_OUT * C_OUT), (C_OUT * 27) ** -0.5, 0.15625),
        "first_bias": scatter_about(seeds[4], (C_OUT,), 0.5, 3.0, (), jnp.float32),
        "second_weight": scatter_about(seeds[5], (27, C_OUT * C_OUT), (C_OUT * 27) ** -0.5, 0.15625),
        "second_bias": scatter_about(seeds[6], (C_OUT,), 0.5, 3.0, (), jnp.float32),
    }


def upsample(padded, weight):
    kernel = jnp.transpose(weight, (1, 0, 2, 3, 4))
    count_d = padded.shape[1] - 2
    count_h = padded.shape[2] - 2
    count_w = padded.shape[3] - 2
    results = []
    for phase_d in range(2):
        for phase_h in range(2):
            for phase_w in range(2):
                taps = kernel[:, :, 3 - phase_d::-2, 3 - phase_h::-2, 3 - phase_w::-2]
                window = padded[:, phase_d:phase_d + count_d + 1, phase_h:phase_h + count_h + 1, phase_w:phase_w + count_w + 1]
                result = lax.conv_general_dilated(window[None], taps, (1, 1, 1), "VALID", dimension_numbers=("NCDHW", "OIDHW", "NCDHW"), preferred_element_type=jnp.float32)[0]
                results.append(result)
    stacked = jnp.stack(results).reshape((2, 2, 2) + results[0].shape)
    stacked = jnp.transpose(stacked, (3, 4, 0, 5, 1, 6, 2))
    return stacked.reshape(stacked.shape[0], 2 * count_d, 2 * count_h, 2 * count_w)


def unpack_conv(weight):
    return jnp.transpose(weight.reshape(3, 3, 3, C_OUT, C_OUT), (3, 4, 0, 1, 2))


def convolve(activation, weight):
    return lax.conv_general_dilated(activation[None], weight, (1, 1, 1), ((1, 1), (1, 1), (1, 1)), dimension_numbers=("NCDHW", "OIDHW", "NCDHW"), preferred_element_type=jnp.float32)[0]


def leaky(value):
    return jnp.where(value > 0, value, 0.2 * value)


def reference(volume, up_weight, up_bias, first_weight, first_bias, second_weight, second_bias):
    cube = volume.reshape(volume.shape[0], volume.shape[1], IN_H, IN_HW)
    up_kernel = up_weight.reshape(up_weight.shape[0], C_OUT, 4, 4, 4)
    padded = jnp.pad(cube, ((0, 0), (1, 1), (1, 1), (1, 1)))
    upsampled = (upsample(padded, up_kernel) + up_bias[:, None, None, None]).astype(jnp.bfloat16)
    hidden = leaky(convolve(upsampled, unpack_conv(first_weight)) + first_bias[:, None, None, None]).astype(jnp.bfloat16)
    decoded = leaky(convolve(hidden, unpack_conv(second_weight)) + second_bias[:, None, None, None]).astype(jnp.bfloat16)
    return decoded
```

```python
import jax
import jax.numpy as jnp
from jax import lax
from jax.experimental import pallas as pl
from jax.experimental.pallas import tpu as pltpu
from jax.sharding import PartitionSpec as P

F32 = jnp.float32
BF16 = jnp.bfloat16
H_IN, W_IN = 16, 64
C = 64
VMEM = pl.BlockSpec(memory_space=pltpu.VMEM)
SMEM = pl.BlockSpec(memory_space=pltpu.SMEM)
NT = (((1,), (1,)), ((), ()))


def params():
    return pltpu.CompilerParams(vmem_limit_bytes=56 * 2**20)


def lanes_of(shape):
    return lax.broadcasted_iota(jnp.int32, shape, len(shape) - 1)


def leaky(value):
    return jnp.where(value > 0, value, 0.2 * value)


def up_weight_kernel(weight_ref, bias_ref, out_ref, rows):
    rows[...] = weight_ref[...].astype(F32).T
    for k in range(64):
        block = rows[pl.ds(k, 32, stride=64), :]
        out_ref[k // 32, pl.ds((k % 32) * 32, 32), :] = block.astype(BF16)
    bias = bias_ref[...]
    high = bias.astype(BF16).astype(F32)
    middle = (bias - high).astype(BF16).astype(F32)
    low = bias - high - middle
    row = lax.broadcasted_iota(jnp.int32, (16, 128), 0)
    parts = jnp.where(row == 0, high, jnp.where(row == 1, middle, jnp.where(row == 2, low, 0.0)))
    for half in range(2):
        out_ref[half, pl.ds(1024, 16), :] = parts.astype(BF16)


def prepare_up(weight, bias_row):
    return pl.pallas_call(
        up_weight_kernel,
        out_shape=jax.ShapeDtypeStruct((2, 1040, 128), BF16),
        in_specs=[VMEM, VMEM],
        out_specs=VMEM,
        scratch_shapes=[pltpu.VMEM((2048, 128), F32)],
        compiler_params=params(),
        cost_estimate=pl.CostEstimate(flops=0, bytes_accessed=4 * 2**20, transcendentals=0),
        name="prepare_up",
    )(weight, bias_row)


def pair_of(taps, index, count):
    zero = jnp.zeros((count, C), BF16)
    low, high = index
    left = taps(low) if 0 <= low < 3 else zero
    right = taps(high) if 0 <= high < 3 else zero
    return jnp.concatenate([left, right], axis=1)


def conv_weight_kernel(first_ref, second_ref, one_ref, two_ref):
    one_ref[...] = jnp.zeros_like(one_ref)
    for eh in range(3):
        for ew in range(3):
            for zo in range(2):
                for zp in range(2):
                    depth = (2 * zp - zo, 2 * zp + 1 - zo)
                    block = pair_of(lambda e: first_ref[9 * e + 3 * eh + ew], depth, C)
                    for b in range(2):
                        wpos = ew + b
                        one_ref[pl.ds(128 * b + 64 * zo, 64), pl.ds(((eh * 2 + zp) * 4 + wpos) * 128, 128)] = block
                    block = pair_of(lambda e: second_ref[9 * e + 3 * eh + ew], depth, 32)
                    two_ref[pl.ds((eh * 3 + ew) * 64 + 32 * zo, 32), pl.ds(zp * 128, 128)] = block


def prepare_convs(first, second):
    return pl.pallas_call(
        conv_weight_kernel,
        out_shape=(jax.ShapeDtypeStruct((256, 3072), BF16), jax.ShapeDtypeStruct((576, 256), BF16)),
        in_specs=[VMEM, VMEM],
        out_specs=(VMEM, VMEM),
        compiler_params=params(),
        cost_estimate=pl.CostEstimate(flops=0, bytes_accessed=4 * 2**20, transcendentals=0),
        name="prepare_convs",
    )(first, second)


def main_kernel(
    place_ref, own_ref, near_ref, far_ref, last_ref, up_own_ref, up_near_ref, up_far_ref,
    one_ref, two_ref, bias_one_ref, bias_two_ref,
    out_ref,
    cells, up_weight, grid, natural, hidden, taps, rows_out,
):
    depth = place_ref[0]
    filt = place_ref[1]
    odd = depth % 2

    low = filt
    up_weight[...] = jnp.zeros_like(up_weight)

    def place_half(source, k_base, count, where_f):
        for k in range(k_base, k_base + count):
            kd, kh, kw = 3 - k // 16, 3 - (k // 4) % 4, 3 - k % 4
            zin, zz = kd // 2, kd % 2
            hk, a = kh // 2, kh % 2
            wk, b = kw // 2, kw % 2
            row = pl.multiple_of(128 * b + 64 * zz + 32 * where_f, 32)
            column = ((hk * 2 + zin) * 3 + wk + b) * 128
            up_weight[a, pl.ds(row, 32), pl.ds(column, 128)] = source(k)

    place_half(lambda k: up_own_ref[k // 32, pl.ds((k % 32) * 32, 32), :], 0, 64, low)
    parity = odd == 0
    place_half(lambda k: jnp.where(parity, up_near_ref[pl.ds(k * 32, 32), :], up_far_ref[pl.ds(k * 32, 32), :]), 0, 32, 1 - low)
    place_half(lambda k: jnp.where(parity, up_far_ref[pl.ds((k - 32) * 32, 32), :], up_near_ref[pl.ds((k - 32) * 32, 32), :]), 32, 32, 1 - low)

    def bias_row(block):
        parts = block.astype(F32)
        return parts[0:1] + parts[1:2] + parts[2:3]

    mine = bias_row(up_own_ref[0, pl.ds(1024, 16), :])
    theirs = bias_row(up_near_ref[pl.ds(1024, 16), :])
    lane = lanes_of((1, 128))
    first_half = (lane // 32) % 2 == 0
    is_low = filt == 0
    bias_up = jnp.where(first_half, jnp.where(is_low, mine, theirs), jnp.where(is_low, theirs, mine))

    cells[...] = jnp.zeros_like(cells)
    width = lax.broadcasted_iota(jnp.int32, (1024, 128), 0) % 64

    def place_plane(plane, index):
        value = plane.astype(F32).T
        before = jnp.where(width == 0, 0.0, pltpu.roll(value, 1, 0))
        after = jnp.where(width == 63, 0.0, pltpu.roll(value, 1023, 0))
        cells[index, pl.ds(64, 1024), 0:128] = before.astype(BF16)
        cells[index, pl.ds(64, 1024), 128:256] = value.astype(BF16)
        cells[index, pl.ds(64, 1024), 256:384] = after.astype(BF16)

    place_plane(own_ref[...], 2)
    place_plane(near_ref[...], 3 - 2 * odd)
    place_plane(far_ref[0], 3 * odd)
    place_plane(far_ref[1], 1 + 3 * odd)
    place_plane(last_ref[...], 4 - 4 * odd)

    grid[0] = jnp.zeros((64, 1536), BF16)
    grid[33] = jnp.zeros((64, 1536), BF16)
    not_first = (depth != 0).astype(F32)
    not_last = (depth != 63).astype(F32)
    half_lane = lane < 64

    for j in range(4):
        left = {0: not_first, 1: 1.0, 2: not_last, 3: 0.0}[j]
        right = {0: 0.0, 1: not_first, 2: 1.0, 3: not_last}[j]
        keep = jnp.where(half_lane, left, right)
        for a in range(2):
            lhs = jnp.concatenate(
                [cells[j + zin, pl.ds((a + hk) * 64, 1024), :] for hk in range(2) for zin in range(2)], axis=1
            )
            total = lax.dot_general(lhs, up_weight[a], NT, preferred_element_type=F32)
            for b in range(2):
                value = (total[:, 128 * b : 128 * b + 128] + bias_up) * keep
                if b == 0:
                    moved = jnp.where(width == 63, 0.0, pltpu.roll(value, 1023, 0))
                else:
                    moved = jnp.where(width == 0, 0.0, pltpu.roll(value, 1, 0))
                for wpos, cube in ((1 + b, value), (3 - 3 * b, moved)):
                    cube = cube.astype(BF16).reshape(16, 64, 128)
                    if j < 3:
                        start = j * 512 + wpos * 128
                        for h in range(16):
                            grid[1 + a + 2 * h, :, start : start + 64] = cube[h, :, 0:64]
                    if j > 0:
                        start = (j - 1) * 512 + wpos * 128 + 64
                        for h in range(16):
                            grid[1 + a + 2 * h, :, start : start + 64] = cube[h, :, 64:128]

    for g in range(2):
        lhs = jnp.concatenate(
            [grid[eh : eh + 32, :, g * 512 : g * 512 + 1024].reshape(2048, 1024) for eh in range(3)], axis=1
        )
        total = lax.dot_general(lhs, one_ref[...], NT, preferred_element_type=F32)
        left = not_first if g == 0 else 1.0
        right = 1.0 if g == 0 else not_last
        keep = jnp.where(half_lane, left, right)
        for b in range(2):
            value = leaky(total[:, 128 * b : 128 * b + 128] + bias_one_ref[...]) * keep
            natural[pl.ds(b, 2048, stride=2), :] = value
        hidden[:, g * 128 : g * 128 + 128] = natural[...].astype(BF16)

    taps[...] = lax.dot_general(two_ref[...], hidden[...], NT, preferred_element_type=F32)
    column = lanes_of((64, 128))
    for h in range(32):
        sums = []
        for ew in range(3):
            terms = [
                taps[pl.ds((eh * 3 + ew) * 64, 64), pl.ds((h + eh - 1) * 128, 128)]
                for eh in range(3)
                if 0 <= h + eh - 1 < 32
            ]
            total = terms[0]
            for term in terms[1:]:
                total = total + term
            sums.append(total)
        value = sums[1]
        value = value + jnp.where(column == 0, 0.0, pltpu.roll(sums[0], 1, 1))
        value = value + jnp.where(column == 127, 0.0, pltpu.roll(sums[2], 127, 1))
        value = leaky(value + bias_two_ref[...])
        for z in range(2):
            rows_out[pl.ds(z * 32 + h, 32, stride=64), :] = value[z * 32 : z * 32 + 32]
    out_ref[...] = rows_out[...].reshape(32, 2, 32, 128).astype(BF16)


def section(place, own, near, far, last, up_own, up_near, up_far, one, two, bias_one, bias_two):
    return pl.pallas_call(
        main_kernel,
        out_shape=jax.ShapeDtypeStruct((32, 2, 32, 128), BF16),
        in_specs=[SMEM] + [VMEM] * 11,
        out_specs=VMEM,
        scratch_shapes=[
            pltpu.VMEM((5, 18 * 64, 384), BF16),
            pltpu.VMEM((2, 256, 1536), BF16),
            pltpu.VMEM((34, 64, 1536), BF16),
            pltpu.VMEM((4096, 128), F32),
            pltpu.VMEM((4096, 256), BF16),
            pltpu.VMEM((576, 4096), F32),
            pltpu.VMEM((2048, 128), F32),
        ],
        compiler_params=params(),
        cost_estimate=pl.CostEstimate(flops=14 * 10**9, bytes_accessed=6 * 2**20, transcendentals=0),
        name="section",
    )(place, own, near, far, last, up_own, up_near, up_far, one, two, bias_one, bias_two)


def shards(volume, up_weight, up_bias, first_weight, first_bias, second_weight, second_bias):
    devices = lax.axis_size("depth")
    depth = lax.axis_index("depth")
    filt = lax.axis_index("filt")
    odd = depth % 2
    swap = [(0, 1), (1, 0)]
    siblings = [(i, i ^ 1) for i in range(devices)]
    across = [(i, i + 1) for i in range(1, devices - 1, 2)]
    across = across + [(j, i) for i, j in across]

    other = lax.ppermute(volume, "filt", swap)
    up_own = prepare_up(up_weight, jnp.tile(up_bias, 4)[None])
    up_near = lax.ppermute(lax.dynamic_index_in_dim(up_own, odd, 0, keepdims=False), "filt", swap)
    up_far = lax.ppermute(up_near, "depth", siblings)

    first = first_weight.reshape(27, C, C)
    second = lax.dynamic_slice_in_dim(second_weight.reshape(27, C, C), filt * 32, 32, 1)
    one, two = prepare_convs(first, second)

    mine = volume.reshape(64, 1024)
    theirs = other.reshape(64, 1024)
    own = jnp.where(filt == 0, jnp.concatenate([mine, theirs]), jnp.concatenate([theirs, mine]))
    near = lax.ppermute(own, "depth", siblings)
    both = jnp.where(odd == 0, jnp.stack([own, near]), jnp.stack([near, own]))
    far = lax.ppermute(both, "depth", across)
    relay = lax.dynamic_index_in_dim(far, 1 - odd, 0, keepdims=False)
    last = lax.ppermute(relay, "depth", siblings)

    place = jnp.stack([depth, filt]).astype(jnp.int32)
    bias_one = jnp.tile(first_bias, 2)[None]
    bias_two = jnp.tile(lax.dynamic_slice_in_dim(second_bias, filt * 32, 32, 0), 2)[:, None]
    bias_two = jnp.broadcast_to(bias_two, (64, 128))
    return section(place, own, near, far, last, up_own, up_near, up_far, one, two, bias_one, bias_two)


def solution(mesh):
    placed = (P("filt", "depth", None), P(None, "filt"), P("filt"), P(), P(), P(), P())
    return jax.shard_map(
        shards,
        mesh=mesh,
        in_specs=placed,
        out_specs=P("filt", "depth", None, None),
        check_vma=False,
    )
```

```python
import jax
import jax.numpy as jnp
from jax import lax
from jax.experimental import pallas as pl
from jax.experimental.pallas import tpu as pltpu
from jax.sharding import PartitionSpec as P


F32 = jnp.float32
BF16 = jnp.bfloat16
VMEM = pl.BlockSpec(memory_space=pltpu.VMEM)
SMEM = pl.BlockSpec(memory_space=pltpu.SMEM)
NT = (((1,), (1,)), ((), ()))


def params(mebibytes):
    return pltpu.CompilerParams(vmem_limit_bytes=mebibytes * 2**20)


def cost(flops, count):
    return pl.CostEstimate(flops=flops, bytes_accessed=count, transcendentals=0)


def lanes_of(shape):
    return lax.broadcasted_iota(jnp.int32, shape, len(shape) - 1)


def leaky(value):
    return jnp.where(value > 0, value, 0.2 * value)


def up_weight_kernel(weight_ref, bias_ref, own_ref, send_ref, rows):
    rows[...] = weight_ref[...].astype(F32).T
    for k in range(64):
        block = rows[pl.ds(k, 32, stride=64), :]
        own_ref[k // 32, pl.ds((k % 32) * 32, 32), :] = block.astype(BF16)
    bias = jnp.concatenate([bias_ref[...]] * 4, axis=1)
    high = bias.astype(BF16).astype(F32)
    middle = (bias - high).astype(BF16).astype(F32)
    low = bias - high - middle
    row = lax.broadcasted_iota(jnp.int32, (16, 128), 0)
    parts = jnp.where(row == 0, high, jnp.where(row == 1, middle, jnp.where(row == 2, low, 0.0)))
    for half in range(2):
        own_ref[half, pl.ds(1024, 16), :] = parts.astype(BF16)
    send_ref[...] = own_ref[lax.axis_index("depth") % 2]


def prepare_up(weight, bias_row):
    return pl.pallas_call(
        up_weight_kernel,
        out_shape=(jax.ShapeDtypeStruct((2, 1040, 128), BF16), jax.ShapeDtypeStruct((1040, 128), BF16)),
        in_specs=[VMEM, VMEM],
        out_specs=(VMEM, VMEM),
        scratch_shapes=[pltpu.VMEM((2048, 128), F32)],
        compiler_params=params(12),
        cost_estimate=cost(10**9, 2 * 2**20),
        name="prepare_up",
    )(weight, bias_row)


def conv_weight_kernel(first_ref, second_ref, one_ref, two_ref, spread):
    lane = lanes_of((1, 128))

    def arrange(source, start, count, out_ref):
        for pair in range(count // 2):
            chunk = source[:, pl.ds(start + pair * 128, 128)].astype(F32)
            spread[pl.ds(2 * pair, 27, stride=64), :] = chunk
            spread[pl.ds(2 * pair + 1, 27, stride=64), :] = pltpu.roll(chunk, 64, 1)
        for eh in range(3):
            for ew in range(3):
                for zp in range(2):
                    for zo in range(2):
                        halves = []
                        for zi in range(2):
                            ed = 2 * zp + zi - zo
                            if 0 <= ed < 3:
                                tap = spread[pl.ds((9 * ed + 3 * eh + ew) * 64, count), :]
                                halves.append(pltpu.roll(tap, 64, 1) if zi else tap)
                            else:
                                halves.append(jnp.zeros((count, 128), F32))
                        block = jnp.where(lane < 64, halves[0], halves[1])
                        row, column = (ew * 2 + zo) * count, (eh * 2 + zp) * 128
                        out_ref[pl.ds(row, count), pl.ds(column, 128)] = block.astype(BF16)

    arrange(first_ref, 0, 64, one_ref)
    arrange(second_ref, pl.multiple_of(lax.axis_index("filt") * 2048, 2048), 32, two_ref)


def prepare_convs(first, second):
    return pl.pallas_call(
        conv_weight_kernel,
        out_shape=(jax.ShapeDtypeStruct((384, 768), BF16), jax.ShapeDtypeStruct((192, 768), BF16)),
        in_specs=[VMEM, VMEM],
        out_specs=(VMEM, VMEM),
        scratch_shapes=[pltpu.VMEM((27 * 64, 128), F32)],
        compiler_params=params(12),
        cost_estimate=cost(10**9, 2 * 2**20),
        name="prepare_convs",
    )(first, second)


def main_kernel(
    own_ref, near_ref, far_ref, last_ref, up_own_ref, up_near_ref, up_far_ref,
    one_ref, two_ref, bias_one_ref, bias_two_ref,
    out_ref,
    cells, up_weight, natural, upsampled, taps, hidden, rows_out,
):
    depth = lax.axis_index("depth")
    filt = lax.axis_index("filt")
    odd = depth % 2
    not_first = (depth != 0).astype(F32)
    not_last = (depth != lax.axis_size("depth") - 1).astype(F32)
    lane = lanes_of((1, 128))

    def place_half(source, where_f, ks):
        for k in ks:
            kd, kh, kw = 3 - k // 16, 3 - (k // 4) % 4, k % 4
            zin, zz = kd // 2, kd % 2
            hk, a = kh // 2, kh % 2
            place = ((3, 0, 1, 2), (2, 1, 0, 3))[zz][kw]
            row = pl.multiple_of(64 * place + 32 * where_f, 32)
            up_weight[a, zz, pl.ds(row, 32), pl.ds((hk * 2 + zin) * 128, 128)] = source(k)

    def part(ref, k):
        return ref[pl.ds((k % 32) * 32, 32), :]

    is_even = odd == 0
    place_half(lambda k: part(up_own_ref.at[k // 32], k), filt, range(64))
    place_half(lambda k: jnp.where(is_even, part(up_near_ref, k), part(up_far_ref, k)), 1 - filt, range(32))
    place_half(lambda k: jnp.where(is_even, part(up_far_ref, k), part(up_near_ref, k)), 1 - filt, range(32, 64))

    def bias_of(block):
        parts = block.astype(F32)
        return parts[0:1] + parts[1:2] + parts[2:3]

    mine = bias_of(up_own_ref[0, pl.ds(1024, 16), :])
    theirs = bias_of(up_near_ref[pl.ds(1024, 16), :])
    is_low = filt == 0
    bias_up = jnp.where(
        (lane // 32) % 2 == 0, jnp.where(is_low, mine, theirs), jnp.where(is_low, theirs, mine)
    )

    def column_of(row):
        return jnp.broadcast_to(row, (128, 128)).T

    row = bias_one_ref[...]
    bias_one = column_of(jnp.concatenate([row, row], axis=1))
    row = bias_two_ref[...]
    row = jnp.where(is_low, row[:, 0:32], row[:, 32:64])
    bias_two = column_of(jnp.concatenate([row] * 4, axis=1))[0:64]

    for i in range(5):
        cells[i, 0:64, :] = jnp.zeros((64, 128), BF16)
        cells[i, 1088:1152, :] = jnp.zeros((64, 128), BF16)

    def place_plane(plane, index):
        cells[index, 64:1088, :] = plane.T

    place_plane(own_ref[...], 2)
    place_plane(near_ref[...], 3 - 2 * odd)
    place_plane(far_ref[0], 3 * odd)
    place_plane(far_ref[1], 1 + 3 * odd)
    place_plane(last_ref[...], 4 - 4 * odd)

    upsampled[0:128, :] = jnp.zeros((128, 384), BF16)
    upsampled[4224:4352, :] = jnp.zeros((128, 384), BF16)
    hidden[:, 0:128] = jnp.zeros((256, 128), BF16)
    hidden[:, 4224:4352] = jnp.zeros((256, 128), BF16)

    width = lax.broadcasted_iota(jnp.int32, (1024, 128), 0) % 64
    low_lanes = lanes_of((1024, 128)) < 64

    for i in range(3):
        keep = (not_first, None, not_last)[i]
        for a in range(2):
            planes = []
            for zz in range(2):
                pair = i + zz
                lhs = jnp.concatenate(
                    [cells[pair + zin, (a + hk) * 64 : (a + hk) * 64 + 1024, :] for hk in range(2) for zin in range(2)],
                    axis=1,
                )
                total = lax.dot_general(lhs, up_weight[a, zz], NT, preferred_element_type=F32)
                aside = total[:, 128:256]
                before = jnp.where(width == 0, 0.0, pltpu.roll(aside, 1, 0))
                after = jnp.where(width == 63, 0.0, pltpu.roll(aside, 1023, 0))
                even_first = low_lanes if zz == 0 else jnp.logical_not(low_lanes)
                value = total[:, 0:128] + jnp.where(even_first, before, after) + bias_up
                planes.append(value if keep is None else value * keep)
            even = jnp.where(low_lanes, planes[0], planes[1])
            uneven = pltpu.roll(jnp.where(low_lanes, planes[1], planes[0]), 64, 1)
            for h in range(16):
                for b, value in ((0, even), (1, uneven)):
                    natural[pl.ds((2 * h + a) * 128 + b, 64, stride=2), :] = value[h * 64 : h * 64 + 64]
        upsampled[128:4224, i * 128 : i * 128 + 128] = natural[...].astype(BF16)

    def combine(count, h):
        where = pl.ds(h * 128, 128)
        column = lanes_of((count, 128))
        value = taps[count : 2 * count, where]
        value = value + jnp.where(column == 0, 0.0, pltpu.roll(taps[0:count, where], 1, 1))
        return value + jnp.where(column == 127, 0.0, pltpu.roll(taps[2 * count : 3 * count, where], 127, 1))

    upper = lax.broadcasted_iota(jnp.int32, (128, 128), 0) < 64
    for g in range(2):
        rhs = jnp.concatenate(
            [upsampled[eh * 128 : eh * 128 + 4096, g * 128 : g * 128 + 256] for eh in range(3)], axis=1
        )
        taps[...] = lax.dot_general(one_ref[...], rhs, NT, preferred_element_type=F32)
        keep = jnp.where(upper, not_first, 1.0) if g == 0 else jnp.where(upper, 1.0, not_last)
        for h in range(32):
            value = leaky(combine(128, h) + bias_one) * keep
            hidden[g * 128 : g * 128 + 128, (h + 1) * 128 : (h + 2) * 128] = value.astype(BF16)

    rhs = jnp.concatenate([hidden[:, eh * 128 : eh * 128 + 4096] for eh in range(3)], axis=0)
    taps[0:192, :] = jnp.dot(two_ref[...], rhs, preferred_element_type=F32)
    for h in range(32):
        value = leaky(combine(64, h) + bias_two)
        for z in range(2):
            rows_out[pl.ds(z * 32 + h, 32, stride=64), :] = value[z * 32 : z * 32 + 32]
    out_ref[...] = rows_out[...].reshape(32, 2, 32, 128).astype(BF16)


def section(*operands):
    return pl.pallas_call(
        main_kernel,
        out_shape=jax.ShapeDtypeStruct((32, 2, 32, 128), BF16),
        in_specs=[VMEM] * 11,
        out_specs=VMEM,
        scratch_shapes=[
            pltpu.VMEM((5, 18 * 64, 128), BF16),
            pltpu.VMEM((2, 2, 256, 512), BF16),
            pltpu.VMEM((4096, 128), F32),
            pltpu.VMEM((34 * 128, 384), BF16),
            pltpu.VMEM((384, 4096), F32),
            pltpu.VMEM((256, 34 * 128), BF16),
            pltpu.VMEM((2048, 128), F32),
        ],
        compiler_params=params(40),
        cost_estimate=cost(10**10, 6 * 2**20),
        name="section",
    )(*operands)


def shards(volume, up_weight, up_bias, first_weight, first_bias, second_weight, second_bias):
    devices = lax.axis_size("depth")
    odd = lax.axis_index("depth") % 2
    filt = lax.axis_index("filt")
    swap = [(0, 1), (1, 0)]
    siblings = [(i, i ^ 1) for i in range(devices)]
    across = [(i, i + 1) for i in range(1, devices - 1, 2)]
    across = across + [(j, i) for i, j in across]

    other = lax.ppermute(volume, "filt", swap)
    up_own, up_send = prepare_up(up_weight, up_bias[None])
    up_near = lax.ppermute(up_send, "filt", swap)
    up_far = lax.ppermute(up_near, "depth", siblings)
    one, two = prepare_convs(first_weight, second_weight)
    mine = volume.reshape(64, 1024)
    theirs = other.reshape(64, 1024)
    own = jnp.where(filt == 0, jnp.concatenate([mine, theirs]), jnp.concatenate([theirs, mine]))
    near = lax.ppermute(own, "depth", siblings)
    both = jnp.where(odd == 0, jnp.stack([own, near]), jnp.stack([near, own]))
    far = lax.ppermute(both, "depth", across)
    relay = lax.dynamic_index_in_dim(far, 1 - odd, 0, keepdims=False)
    last = lax.ppermute(relay, "depth", siblings)
    return section(
        own, near, far, last, up_own, up_near, up_far, one, two, first_bias[None], second_bias[None]
    )


def solution(mesh):
    placed = (P("filt", "depth", None), P(None, "filt"), P("filt"), P(), P(), P(), P())
    return jax.shard_map(
        shards,
        mesh=mesh,
        in_specs=placed,
        out_specs=P("filt", "depth", None, None),
        check_vma=False,
    )
```

```python
import jax
import jax.numpy as jnp
from jax import lax
from jax.experimental import pallas as pl
from jax.experimental.pallas import tpu as pltpu
from jax.sharding import PartitionSpec as P


F32 = jnp.float32
BF16 = jnp.bfloat16
VMEM = pl.BlockSpec(memory_space=pltpu.VMEM)
SMEM = pl.BlockSpec(memory_space=pltpu.SMEM)
NT = (((1,), (1,)), ((), ()))


def params(mebibytes):
    return pltpu.CompilerParams(vmem_limit_bytes=mebibytes * 2**20)


def cost(flops, count):
    return pl.CostEstimate(flops=flops, bytes_accessed=count, transcendentals=0)


def lanes_of(shape):
    return lax.broadcasted_iota(jnp.int32, shape, len(shape) - 1)


def leaky(value):
    return jnp.where(value > 0, value, 0.2 * value)


def up_weight_kernel(weight_ref, bias_ref, own_ref, send_ref, rows):
    rows[...] = weight_ref[...].astype(F32).T
    for k in range(64):
        block = rows[pl.ds(k, 32, stride=64), :]
        own_ref[k // 32, pl.ds((k % 32) * 32, 32), :] = block.astype(BF16)
    bias = jnp.concatenate([bias_ref[...]] * 4, axis=1)
    high = bias.astype(BF16).astype(F32)
    middle = (bias - high).astype(BF16).astype(F32)
    low = bias - high - middle
    row = lax.broadcasted_iota(jnp.int32, (16, 128), 0)
    parts = jnp.where(row == 0, high, jnp.where(row == 1, middle, jnp.where(row == 2, low, 0.0)))
    for half in range(2):
        own_ref[half, pl.ds(1024, 16), :] = parts.astype(BF16)
    send_ref[...] = own_ref[lax.axis_index("depth") % 2]


def prepare_up(weight, bias_row):
    return pl.pallas_call(
        up_weight_kernel,
        out_shape=(jax.ShapeDtypeStruct((2, 1040, 128), BF16), jax.ShapeDtypeStruct((1040, 128), BF16)),
        in_specs=[VMEM, VMEM],
        out_specs=(VMEM, VMEM),
        scratch_shapes=[pltpu.VMEM((2048, 128), F32)],
        compiler_params=params(12),
        cost_estimate=cost(10**9, 2 * 2**20),
        name="prepare_up",
    )(weight, bias_row)


def conv_weight_kernel(first_ref, second_ref, one_ref, two_ref, spread):
    odd = lax.axis_index("depth") % 2
    lane = lanes_of((1, 128))

    def arrange(source, start, count, out_ref):
        for pair in range(count // 2):
            chunk = source[:, pl.ds(start + pair * 128, 128)].astype(F32)
            spread[pl.ds(2 * pair, 27, stride=64), :] = chunk
            spread[pl.ds(2 * pair + 1, 27, stride=64), :] = pltpu.roll(chunk, 64, 1)
        for eh in range(3):
            for ew in range(3):
                for zp in range(2):
                    for zo in range(2):
                        halves = []
                        for zi in range(2):
                            ed = 2 * zp + zi - zo
                            if 0 <= ed < 3:
                                ed = ed + odd * (2 - 2 * ed)
                                start_row = pl.multiple_of((9 * ed + 3 * eh + ew) * 64, 64)
                                tap = spread[pl.ds(start_row, count), :]
                                halves.append(pltpu.roll(tap, 64, 1) if zi else tap)
                            else:
                                halves.append(jnp.zeros((count, 128), F32))
                        block = jnp.where(lane < 64, halves[0], halves[1])
                        row, column = (ew * 2 + zo) * count, (eh * 2 + zp) * 128
                        out_ref[pl.ds(row, count), pl.ds(column, 128)] = block.astype(BF16)

    arrange(first_ref, 0, 64, one_ref)
    arrange(second_ref, pl.multiple_of(lax.axis_index("filt") * 2048, 2048), 32, two_ref)


def prepare_convs(first, second):
    return pl.pallas_call(
        conv_weight_kernel,
        out_shape=(jax.ShapeDtypeStruct((384, 768), BF16), jax.ShapeDtypeStruct((192, 768), BF16)),
        in_specs=[VMEM, VMEM],
        out_specs=(VMEM, VMEM),
        scratch_shapes=[pltpu.VMEM((27 * 64, 128), F32)],
        compiler_params=params(12),
        cost_estimate=cost(10**9, 2 * 2**20),
        name="prepare_convs",
    )(first, second)


def has_chip_beside():
    depth = lax.axis_index("depth")
    outside = (depth == 0) | (depth == lax.axis_size("depth") - 1)
    return jnp.where(outside, 0.0, 1.0).astype(F32)


def place_plane(plane, ref):
    ref[0:64, :] = jnp.zeros((64, 128), BF16)
    ref[64:1088, :] = plane.T
    ref[1088:1152, :] = jnp.zeros((64, 128), BF16)


def upsample(low_ref, high_ref, weight_ref, bias, zz, a):
    start = a * 64
    lhs = jnp.concatenate(
        [ref[start + hk * 64 : start + hk * 64 + 1024, :] for hk in range(2) for ref in (low_ref, high_ref)], axis=1
    )
    total = lax.dot_general(lhs, weight_ref[a, zz], NT, preferred_element_type=F32)
    width = lax.broadcasted_iota(jnp.int32, (1024, 128), 0) % 64
    aside = total[:, 128:256]
    before = jnp.where(width == 0, 0.0, pltpu.roll(aside, 1, 0))
    after = jnp.where(width == 63, 0.0, pltpu.roll(aside, 1023, 0))
    low_lanes = lanes_of((1024, 128)) < 64
    pair = (before, after) if zz == 0 else (after, before)
    return total[:, 0:128] + jnp.where(low_lanes, *pair) + bias


def interleave(low, high, a, natural):
    low_lanes = lanes_of((1024, 128)) < 64
    even = jnp.where(low_lanes, low, high)
    uneven = pltpu.roll(jnp.where(low_lanes, high, low), 64, 1)
    for h in range(16):
        for b, value in ((0, even), (1, uneven)):
            natural[pl.ds((2 * h + a) * 128 + b, 64, stride=2), :] = value[h * 64 : h * 64 + 64]


def place_pair(natural, ref):
    ref[0:128, :] = jnp.zeros((128, 128), BF16)
    ref[128:4224, :] = natural[...].astype(BF16)
    ref[4224:4352, :] = jnp.zeros((128, 128), BF16)


def column_of(row):
    return jnp.broadcast_to(row, (128, 128)).T


def combine(taps, count, h):
    where = pl.ds(h * 128, 128)
    column = lanes_of((count, 128))
    value = taps[count : 2 * count, where]
    value = value + jnp.where(column == 0, 0.0, pltpu.roll(taps[0:count, where], 1, 1))
    return value + jnp.where(column == 127, 0.0, pltpu.roll(taps[2 * count : 3 * count, where], 127, 1))


def hide(pairs, weight_ref, bias_ref, taps, keep, ref):
    rhs = jnp.concatenate([pair[eh * 128 : eh * 128 + 4096, :] for eh in range(3) for pair in pairs], axis=1)
    taps[...] = lax.dot_general(weight_ref[...], rhs, NT, preferred_element_type=F32)
    row = bias_ref[...]
    bias = column_of(jnp.concatenate([row, row], axis=1))
    ref[:, 0:128] = jnp.zeros((128, 128), BF16)
    ref[:, 4224:4352] = jnp.zeros((128, 128), BF16)
    for h in range(32):
        value = leaky(combine(taps, 128, h) + bias)
        if keep is not None:
            value = value * keep
        ref[:, (h + 1) * 128 : (h + 2) * 128] = value.astype(BF16)


def start_kernel(own_ref, near_ref, up_own_ref, up_near_ref, up_far_ref, up_weight, bias_ref, cells, kept):
    odd = lax.axis_index("depth") % 2
    filt = lax.axis_index("filt")

    for k in range(64):
        kd, kh, kw = 3 - k // 16, 3 - (k // 4) % 4, k % 4
        zin, zz = kd // 2, kd % 2
        hk, a = kh // 2, kh % 2
        place = ((3, 0, 1, 2), (2, 1, 0, 3))[zz][kw]
        half, rest = k // 32, k % 16
        source = pl.ds(pl.multiple_of(((k // 16 % 2 + odd) % 2 * 16 + rest) * 32, 32), 32)
        column = pl.ds((hk * 2 + zin) * 128, 128)
        mine = up_own_ref[(half + odd) % 2, source, :]
        up_weight[a, zz, pl.ds(pl.multiple_of(64 * place + 32 * filt, 32), 32), column] = mine
        theirs = (up_near_ref, up_far_ref)[half][source, :]
        up_weight[a, zz, pl.ds(pl.multiple_of(64 * place + 32 - 32 * filt, 32), 32), column] = theirs

    def bias_of(block):
        parts = block.astype(F32)
        return parts[0:1] + parts[1:2] + parts[2:3]

    mine = bias_of(up_own_ref[0, pl.ds(1024, 16), :])
    theirs = bias_of(up_near_ref[pl.ds(1024, 16), :])
    is_mine = (lanes_of((1, 128)) // 32) % 2 == filt
    bias = jnp.where(is_mine, mine, theirs)
    bias_ref[...] = jnp.broadcast_to(bias, (8, 128))

    place_plane(own_ref[...], cells.at[0])
    place_plane(near_ref[...], cells.at[1])
    for zz in range(2):
        for a in range(2):
            kept[zz, a] = upsample(cells.at[0], cells.at[1], up_weight, bias, zz, a).astype(BF16)


def middle_kernel(far_ref, cells, kept, up_weight, bias_ref, one_ref, bias_one_ref, pair_ref, hidden, near, edge, first, natural, taps):
    keep = has_chip_beside()
    place_plane(far_ref[0], near)
    place_plane(far_ref[1], edge)
    bias = bias_ref[0:1]
    for a in range(2):
        low = upsample(edge, near, up_weight, bias, 0, a) * keep
        high = upsample(near, cells.at[0], up_weight, bias, 1, a) * keep
        interleave(low, high, a, natural)
    place_pair(natural, first)
    for a in range(2):
        low = upsample(near, cells.at[0], up_weight, bias, 0, a)
        interleave(low, kept[1, a].astype(F32), a, natural)
    place_pair(natural, pair_ref)
    upper = lax.broadcasted_iota(jnp.int32, (128, 128), 0) < 64
    hide((first, pair_ref), one_ref, bias_one_ref, taps, jnp.where(upper, keep, 1.0), hidden)


def end_kernel(
    last_ref, cells, kept, up_weight, bias_ref, pair_ref, hidden_ref, one_ref, two_ref, bias_one_ref, bias_two_ref,
    out_ref,
    edge, second, natural, taps, hidden, rows_out,
):
    odd = lax.axis_index("depth") % 2
    place_plane(last_ref[...], edge)
    bias = bias_ref[0:1]
    for a in range(2):
        high = upsample(cells.at[1], edge, up_weight, bias, 1, a)
        interleave(kept[0, a].astype(F32), high, a, natural)
    place_pair(natural, second)
    hide((pair_ref, second), one_ref, bias_one_ref, taps, None, hidden)

    rhs = jnp.concatenate(
        [ref[:, eh * 128 : eh * 128 + 4096] for eh in range(3) for ref in (hidden_ref, hidden)], axis=0
    )
    taps[0:192, :] = jnp.dot(two_ref[...], rhs, preferred_element_type=F32)
    row = bias_two_ref[...]
    row = jnp.where(lax.axis_index("filt") == 0, row[:, 0:32], row[:, 32:64])
    bias = column_of(jnp.concatenate([row] * 4, axis=1))[0:64]
    for h in range(32):
        value = leaky(combine(taps, 64, h) + bias)
        for z in range(2):
            rows_out[pl.ds((z + odd) % 2 * 32 + h, 32, stride=64), :] = value[z * 32 : z * 32 + 32]
    out_ref[...] = rows_out[...].reshape(32, 2, 32, 128).astype(BF16)


def start(*operands):
    return pl.pallas_call(
        start_kernel,
        out_shape=(
            jax.ShapeDtypeStruct((2, 2, 256, 512), BF16),
            jax.ShapeDtypeStruct((8, 128), F32),
            jax.ShapeDtypeStruct((2, 1152, 128), BF16),
            jax.ShapeDtypeStruct((2, 2, 1024, 128), BF16),
        ),
        in_specs=[VMEM] * 5,
        out_specs=(VMEM,) * 4,
        compiler_params=params(16),
        cost_estimate=cost(2 * 10**9, 4 * 2**20),
        name="start",
    )(*operands)


def middle(*operands):
    return pl.pallas_call(
        middle_kernel,
        out_shape=(jax.ShapeDtypeStruct((4352, 128), BF16), jax.ShapeDtypeStruct((128, 4352), BF16)),
        in_specs=[VMEM] * 7,
        out_specs=(VMEM,) * 2,
        scratch_shapes=[
            pltpu.VMEM((1152, 128), BF16),
            pltpu.VMEM((1152, 128), BF16),
            pltpu.VMEM((4352, 128), BF16),
            pltpu.VMEM((4096, 128), F32),
            pltpu.VMEM((384, 4096), F32),
        ],
        compiler_params=params(28),
        cost_estimate=cost(5 * 10**9, 4 * 2**20),
        name="middle",
    )(*operands)


def end(*operands):
    return pl.pallas_call(
        end_kernel,
        out_shape=jax.ShapeDtypeStruct((32, 2, 32, 128), BF16),
        in_specs=[VMEM] * 11,
        out_specs=VMEM,
        scratch_shapes=[
            pltpu.VMEM((1152, 128), BF16),
            pltpu.VMEM((4352, 128), BF16),
            pltpu.VMEM((4096, 128), F32),
            pltpu.VMEM((384, 4096), F32),
            pltpu.VMEM((128, 4352), BF16),
            pltpu.VMEM((2048, 128), F32),
        ],
        compiler_params=params(28),
        cost_estimate=cost(5 * 10**9, 4 * 2**20),
        name="end",
    )(*operands)


def shards(volume, up_weight, up_bias, first_weight, first_bias, second_weight, second_bias):
    devices = lax.axis_size("depth")
    filt = lax.axis_index("filt")
    swap = [(0, 1), (1, 0)]
    siblings = [(i, i ^ 1) for i in range(devices)]
    across = [(i, i + 1) for i in range(1, devices - 1, 2)]
    across = across + [(j, i) for i, j in across]

    other = lax.ppermute(volume, "filt", swap)
    up_own, up_send = prepare_up(up_weight, up_bias[None])
    up_near = lax.ppermute(up_send, "filt", swap)
    up_far = lax.ppermute(up_near, "depth", siblings)
    one, two = prepare_convs(first_weight, second_weight)
    mine = volume.reshape(64, 1024)
    theirs = other.reshape(64, 1024)
    own = jnp.where(filt == 0, jnp.concatenate([mine, theirs]), jnp.concatenate([theirs, mine]))
    near = lax.ppermute(own, "depth", siblings)
    far = lax.ppermute(jnp.stack([own, near]), "depth", across)
    last = lax.ppermute(far[0], "depth", siblings)
    weight, bias, cells, kept = start(own, near, up_own, up_near, up_far)
    pair, hidden = middle(far, cells, kept, weight, bias, one, first_bias[None])
    return end(
        last, cells, kept, weight, bias, pair, hidden, one, two, first_bias[None], second_bias[None]
    )


def solution(mesh):
    placed = (P("filt", "depth", None), P(None, "filt"), P("filt"), P(), P(), P(), P())
    return jax.shard_map(
        shards,
        mesh=mesh,
        in_specs=placed,
        out_specs=P("filt", "depth", None, None),
        check_vma=False,
    )
```

```python
import jax
import jax.numpy as jnp
from jax import lax
from jax.experimental import pallas as pl
from jax.experimental.pallas import tpu as pltpu
from jax.sharding import PartitionSpec as P


F32 = jnp.float32
BF16 = jnp.bfloat16
VMEM = pl.BlockSpec(memory_space=pltpu.VMEM)
SMEM = pl.BlockSpec(memory_space=pltpu.SMEM)
NT = (((1,), (1,)), ((), ()))


def params(mebibytes):
    return pltpu.CompilerParams(vmem_limit_bytes=mebibytes * 2**20)


def cost(flops, count):
    return pl.CostEstimate(flops=flops, bytes_accessed=count, transcendentals=0)


def lanes_of(shape):
    return lax.broadcasted_iota(jnp.int32, shape, len(shape) - 1)


def leaky(value):
    return jnp.where(value > 0, value, 0.2 * value)


def up_weight_kernel(weight_ref, bias_ref, own_ref, send_ref, rows):
    rows[...] = weight_ref[...].astype(F32).T
    for k in range(64):
        block = rows[pl.ds(k, 32, stride=64), :]
        own_ref[k // 32, pl.ds((k % 32) * 32, 32), :] = block.astype(BF16)
    bias = jnp.concatenate([bias_ref[...]] * 4, axis=1)
    high = bias.astype(BF16).astype(F32)
    middle = (bias - high).astype(BF16).astype(F32)
    low = bias - high - middle
    row = lax.broadcasted_iota(jnp.int32, (16, 128), 0)
    parts = jnp.where(row == 0, high, jnp.where(row == 1, middle, jnp.where(row == 2, low, 0.0)))
    for half in range(2):
        own_ref[half, pl.ds(1024, 16), :] = parts.astype(BF16)
    send_ref[...] = own_ref[lax.axis_index("depth") % 2]


def prepare_up(weight, bias_row):
    return pl.pallas_call(
        up_weight_kernel,
        out_shape=(jax.ShapeDtypeStruct((2, 1040, 128), BF16), jax.ShapeDtypeStruct((1040, 128), BF16)),
        in_specs=[VMEM, VMEM],
        out_specs=(VMEM, VMEM),
        scratch_shapes=[pltpu.VMEM((2048, 128), F32)],
        compiler_params=params(12),
        cost_estimate=cost(10**9, 2 * 2**20),
        name="prepare_up",
    )(weight, bias_row)


def conv_weight_kernel(first_ref, second_ref, one_ref, two_ref, spread):
    odd = lax.axis_index("depth") % 2
    lane = lanes_of((1, 128))

    def arrange(source, start, count, out_ref):
        for pair in range(count // 2):
            chunk = source[:, pl.ds(start + pair * 128, 128)].astype(F32)
            spread[pl.ds(2 * pair, 27, stride=64), :] = chunk
            spread[pl.ds(2 * pair + 1, 27, stride=64), :] = pltpu.roll(chunk, 64, 1)
        for eh in range(3):
            for ew in range(3):
                for zp in range(2):
                    for zo in range(2):
                        halves = []
                        for zi in range(2):
                            ed = 2 * zp + zi - zo
                            if 0 <= ed < 3:
                                ed = ed + odd * (2 - 2 * ed)
                                start_row = pl.multiple_of((9 * ed + 3 * eh + ew) * 64, 64)
                                tap = spread[pl.ds(start_row, count), :]
                                halves.append(pltpu.roll(tap, 64, 1) if zi else tap)
                            else:
                                halves.append(jnp.zeros((count, 128), F32))
                        block = jnp.where(lane < 64, halves[0], halves[1])
                        row, column = (ew * 2 + zo) * count, (eh * 2 + zp) * 128
                        out_ref[pl.ds(row, count), pl.ds(column, 128)] = block.astype(BF16)

    arrange(first_ref, 0, 64, one_ref)
    arrange(second_ref, pl.multiple_of(lax.axis_index("filt") * 2048, 2048), 32, two_ref)


def prepare_convs(first, second):
    return pl.pallas_call(
        conv_weight_kernel,
        out_shape=(jax.ShapeDtypeStruct((384, 768), BF16), jax.ShapeDtypeStruct((192, 768), BF16)),
        in_specs=[VMEM, VMEM],
        out_specs=(VMEM, VMEM),
        scratch_shapes=[pltpu.VMEM((27 * 64, 128), F32)],
        compiler_params=params(12),
        cost_estimate=cost(10**9, 2 * 2**20),
        name="prepare_convs",
    )(first, second)


def has_chip_beside():
    depth = lax.axis_index("depth")
    outside = (depth == 0) | (depth == lax.axis_size("depth") - 1)
    return jnp.where(outside, 0.0, 1.0).astype(F32)


def place_plane(plane, ref):
    ref[0:64, :] = jnp.zeros((64, 128), BF16)
    ref[64:1088, :] = plane.T
    ref[1088:1152, :] = jnp.zeros((64, 128), BF16)


def upsample(low_ref, high_ref, weight_ref, bias, zz, a):
    start = a * 64
    lhs = jnp.concatenate(
        [ref[start + hk * 64 : start + hk * 64 + 1024, :] for hk in range(2) for ref in (low_ref, high_ref)], axis=1
    )
    total = lax.dot_general(lhs, weight_ref[a, zz], NT, preferred_element_type=F32)
    width = lax.broadcasted_iota(jnp.int32, (1024, 128), 0) % 64
    aside = total[:, 128:256]
    before = jnp.where(width == 0, 0.0, pltpu.roll(aside, 1, 0))
    after = jnp.where(width == 63, 0.0, pltpu.roll(aside, 1023, 0))
    low_lanes = lanes_of((1024, 128)) < 64
    pair = (before, after) if zz == 0 else (after, before)
    return total[:, 0:128] + jnp.where(low_lanes, *pair) + bias


def interleave(low, high, a, natural):
    low_lanes = lanes_of((1024, 128)) < 64
    even = jnp.where(low_lanes, low, high)
    uneven = pltpu.roll(jnp.where(low_lanes, high, low), 64, 1)
    for h in range(16):
        for b, value in ((0, even), (1, uneven)):
            natural[pl.ds((2 * h + a) * 128 + b, 64, stride=2), :] = value[h * 64 : h * 64 + 64]


def place_pair(natural, ref):
    ref[0:128, :] = jnp.zeros((128, 128), BF16)
    ref[128:4224, :] = natural[...].astype(BF16)
    ref[4224:4352, :] = jnp.zeros((128, 128), BF16)


def column_of(row):
    return jnp.broadcast_to(row, (128, 128)).T


def combine(taps, count, h):
    where = pl.ds(h * 128, 128)
    column = lanes_of((count, 128))
    value = taps[count : 2 * count, where]
    value = value + jnp.where(column == 0, 0.0, pltpu.roll(taps[0:count, where], 1, 1))
    return value + jnp.where(column == 127, 0.0, pltpu.roll(taps[2 * count : 3 * count, where], 127, 1))


def hide(pairs, weight_ref, bias_ref, taps, keep, ref):
    rhs = jnp.concatenate([pair[eh * 128 : eh * 128 + 4096, :] for eh in range(3) for pair in pairs], axis=1)
    taps[...] = lax.dot_general(weight_ref[...], rhs, NT, preferred_element_type=F32)
    row = bias_ref[...]
    bias = column_of(jnp.concatenate([row, row], axis=1))
    ref[:, 0:128] = jnp.zeros((128, 128), BF16)
    ref[:, 4224:4352] = jnp.zeros((128, 128), BF16)
    for h in range(32):
        value = leaky(combine(taps, 128, h) + bias)
        if keep is not None:
            value = value * keep
        ref[:, (h + 1) * 128 : (h + 2) * 128] = value.astype(BF16)


def start_kernel(own_ref, near_ref, up_own_ref, up_near_ref, up_far_ref, up_weight, bias_ref, cells, kept):
    odd = lax.axis_index("depth") % 2
    filt = lax.axis_index("filt")

    for k in range(64):
        kd, kh, kw = 3 - k // 16, 3 - (k // 4) % 4, k % 4
        zin, zz = kd // 2, kd % 2
        hk, a = kh // 2, kh % 2
        place = ((3, 0, 1, 2), (2, 1, 0, 3))[zz][kw]
        half, rest = k // 32, k % 16
        source = pl.ds(pl.multiple_of(((k // 16 % 2 + odd) % 2 * 16 + rest) * 32, 32), 32)
        column = pl.ds((hk * 2 + zin) * 128, 128)
        mine = up_own_ref[(half + odd) % 2, source, :]
        up_weight[a, zz, pl.ds(pl.multiple_of(64 * place + 32 * filt, 32), 32), column] = mine
        theirs = (up_near_ref, up_far_ref)[half][source, :]
        up_weight[a, zz, pl.ds(pl.multiple_of(64 * place + 32 - 32 * filt, 32), 32), column] = theirs

    def bias_of(block):
        parts = block.astype(F32)
        return parts[0:1] + parts[1:2] + parts[2:3]

    mine = bias_of(up_own_ref[0, pl.ds(1024, 16), :])
    theirs = bias_of(up_near_ref[pl.ds(1024, 16), :])
    is_mine = (lanes_of((1, 128)) // 32) % 2 == filt
    bias = jnp.where(is_mine, mine, theirs)
    bias_ref[...] = jnp.broadcast_to(bias, (8, 128))

    place_plane(own_ref[...], cells.at[0])
    place_plane(near_ref[...], cells.at[1])
    for zz in range(2):
        for a in range(2):
            kept[zz, a] = upsample(cells.at[0], cells.at[1], up_weight, bias, zz, a).astype(BF16)


def middle_kernel(next_ref, cells, kept, up_weight, bias_ref, near, pair_ref, low_kept, natural):
    place_plane(next_ref[...], near)
    bias = bias_ref[0:1]
    for a in range(2):
        low_kept[a] = upsample(near, cells.at[0], up_weight, bias, 1, a).astype(BF16)
        low = upsample(near, cells.at[0], up_weight, bias, 0, a)
        interleave(low, kept[1, a].astype(F32), a, natural)
    place_pair(natural, pair_ref)


def late_kernel(
    last_ref, cells, kept, up_weight, bias_ref, pair_ref, one_ref, bias_one_ref,
    hidden,
    edge, second, natural, taps,
):
    place_plane(last_ref[...], edge)
    bias = bias_ref[0:1]
    for a in range(2):
        high = upsample(cells.at[1], edge, up_weight, bias, 1, a)
        interleave(kept[0, a].astype(F32), high, a, natural)
    place_pair(natural, second)
    hide((pair_ref, second), one_ref, bias_one_ref, taps, None, hidden)


def end_kernel(
    after_ref, near, low_kept, up_weight, bias_ref, pair_ref, hidden_ref, one_ref, two_ref, bias_one_ref, bias_two_ref,
    out_ref,
    edge, first, natural, taps, hidden, rows_out,
):
    odd = lax.axis_index("depth") % 2
    keep = has_chip_beside()
    place_plane(after_ref[...], edge)
    bias = bias_ref[0:1]
    for a in range(2):
        low = upsample(edge, near, up_weight, bias, 0, a) * keep
        interleave(low, low_kept[a].astype(F32) * keep, a, natural)
    place_pair(natural, first)
    upper = lax.broadcasted_iota(jnp.int32, (128, 128), 0) < 64
    hide((first, pair_ref), one_ref, bias_one_ref, taps, jnp.where(upper, keep, 1.0), hidden)

    rhs = jnp.concatenate(
        [ref[:, eh * 128 : eh * 128 + 4096] for eh in range(3) for ref in (hidden, hidden_ref)], axis=0
    )
    taps[0:192, :] = jnp.dot(two_ref[...], rhs, preferred_element_type=F32)
    row = bias_two_ref[...]
    row = jnp.where(lax.axis_index("filt") == 0, row[:, 0:32], row[:, 32:64])
    bias = column_of(jnp.concatenate([row] * 4, axis=1))[0:64]
    for h in range(32):
        value = leaky(combine(taps, 64, h) + bias)
        for z in range(2):
            rows_out[pl.ds((z + odd) % 2 * 32 + h, 32, stride=64), :] = value[z * 32 : z * 32 + 32]
    out_ref[...] = rows_out[...].reshape(32, 2, 32, 128).astype(BF16)


def start(*operands):
    return pl.pallas_call(
        start_kernel,
        out_shape=(
            jax.ShapeDtypeStruct((2, 2, 256, 512), BF16),
            jax.ShapeDtypeStruct((8, 128), F32),
            jax.ShapeDtypeStruct((2, 1152, 128), BF16),
            jax.ShapeDtypeStruct((2, 2, 1024, 128), BF16),
        ),
        in_specs=[VMEM] * 5,
        out_specs=(VMEM,) * 4,
        compiler_params=params(16),
        cost_estimate=cost(2 * 10**9, 4 * 2**20),
        name="start",
    )(*operands)


def middle(*operands):
    return pl.pallas_call(
        middle_kernel,
        out_shape=(
            jax.ShapeDtypeStruct((1152, 128), BF16),
            jax.ShapeDtypeStruct((4352, 128), BF16),
            jax.ShapeDtypeStruct((2, 1024, 128), BF16),
        ),
        in_specs=[VMEM] * 5,
        out_specs=(VMEM,) * 3,
        scratch_shapes=[pltpu.VMEM((4096, 128), F32)],
        compiler_params=params(16),
        cost_estimate=cost(2 * 10**9, 4 * 2**20),
        name="middle",
    )(*operands)


def late(*operands):
    return pl.pallas_call(
        late_kernel,
        out_shape=jax.ShapeDtypeStruct((128, 4352), BF16),
        in_specs=[VMEM] * 8,
        out_specs=VMEM,
        scratch_shapes=[
            pltpu.VMEM((1152, 128), BF16),
            pltpu.VMEM((4352, 128), BF16),
            pltpu.VMEM((4096, 128), F32),
            pltpu.VMEM((384, 4096), F32),
        ],
        compiler_params=params(28),
        cost_estimate=cost(5 * 10**9, 4 * 2**20),
        name="late",
    )(*operands)


def end(*operands):
    return pl.pallas_call(
        end_kernel,
        out_shape=jax.ShapeDtypeStruct((32, 2, 32, 128), BF16),
        in_specs=[VMEM] * 11,
        out_specs=VMEM,
        scratch_shapes=[
            pltpu.VMEM((1152, 128), BF16),
            pltpu.VMEM((4352, 128), BF16),
            pltpu.VMEM((4096, 128), F32),
            pltpu.VMEM((384, 4096), F32),
            pltpu.VMEM((128, 4352), BF16),
            pltpu.VMEM((2048, 128), F32),
        ],
        compiler_params=params(28),
        cost_estimate=cost(5 * 10**9, 4 * 2**20),
        name="end",
    )(*operands)


def shards(volume, up_weight, up_bias, first_weight, first_bias, second_weight, second_bias):
    devices = lax.axis_size("depth")
    filt = lax.axis_index("filt")
    swap = [(0, 1), (1, 0)]
    siblings = [(i, i ^ 1) for i in range(devices)]
    across = [(i, i + 1) for i in range(1, devices - 1, 2)]
    across = across + [(j, i) for i, j in across]

    mine = volume.reshape(64, 1024)
    theirs = lax.ppermute(mine, "filt", swap)
    up_own, up_send = prepare_up(up_weight, up_bias[None])
    up_near = lax.ppermute(up_send, "filt", swap)
    own = jnp.where(filt == 0, jnp.concatenate([mine, theirs]), jnp.concatenate([theirs, mine]))
    beyond = lax.ppermute(own, "depth", across)
    near = lax.ppermute(own, "depth", siblings)
    after = lax.ppermute(near, "depth", across)
    up_far = lax.ppermute(up_near, "depth", siblings)
    last = lax.ppermute(beyond, "depth", siblings)
    one, two = prepare_convs(first_weight, second_weight)
    weight, bias, cells, kept = start(own, near, up_own, up_near, up_far)
    next_cells, pair, low_kept = middle(beyond, cells, kept, weight, bias)
    hidden = late(last, cells, kept, weight, bias, pair, one, first_bias[None])
    return end(after, next_cells, low_kept, weight, bias, pair, hidden, one, two, first_bias[None], second_bias[None])


def solution(mesh):
    placed = (P("filt", "depth", None), P(None, "filt"), P("filt"), P(), P(), P(), P())
    return jax.shard_map(
        shards,
        mesh=mesh,
        in_specs=placed,
        out_specs=P("filt", "depth", None, None),
        check_vma=False,
    )
```

```python
import jax
import jax.numpy as jnp
from jax import lax
from jax.experimental import pallas as pl
from jax.experimental.pallas import tpu as pltpu
from jax.sharding import PartitionSpec as P


F32 = jnp.float32
BF16 = jnp.bfloat16
STEP = 72
VMEM = pl.BlockSpec(memory_space=pltpu.VMEM)
SMEM = pl.BlockSpec(memory_space=pltpu.SMEM)
NT = (((1,), (1,)), ((), ()))


def params(mebibytes):
    return pltpu.CompilerParams(vmem_limit_bytes=mebibytes * 2**20)


def cost(flops, count):
    return pl.CostEstimate(flops=flops, bytes_accessed=count, transcendentals=0)


def lanes_of(shape):
    return lax.broadcasted_iota(jnp.int32, shape, len(shape) - 1)


def leaky(value):
    return jnp.maximum(value, 0.2 * value)


def up_weight_kernel(weight_ref, bias_ref, own_ref, send_ref, rows):
    turned = weight_ref[...].astype(F32).T
    for o in range(32):
        rows[o * STEP : o * STEP + 64, :] = turned[o * 64 : o * 64 + 64]
    for k in range(64):
        block = rows[pl.ds(k, 32, stride=STEP), :]
        own_ref[k // 32, pl.ds((k % 32) * 32, 32), :] = block.astype(BF16)
    bias = jnp.concatenate([bias_ref[...]] * 4, axis=1)
    high = bias.astype(BF16).astype(F32)
    middle = (bias - high).astype(BF16).astype(F32)
    low = bias - high - middle
    row = lax.broadcasted_iota(jnp.int32, (16, 128), 0)
    parts = jnp.where(row == 0, high, jnp.where(row == 1, middle, jnp.where(row == 2, low, 0.0)))
    for half in range(2):
        own_ref[half, pl.ds(1024, 16), :] = parts.astype(BF16)
    send_ref[...] = own_ref[lax.axis_index("depth") % 2]


def prepare_up(weight, bias_row):
    return pl.pallas_call(
        up_weight_kernel,
        out_shape=(jax.ShapeDtypeStruct((2, 1040, 128), BF16), jax.ShapeDtypeStruct((1040, 128), BF16)),
        in_specs=[VMEM, VMEM],
        out_specs=(VMEM, VMEM),
        scratch_shapes=[pltpu.VMEM((32 * STEP, 128), F32)],
        compiler_params=params(12),
        cost_estimate=cost(10**9, 2 * 2**20),
        name="prepare_up",
    )(weight, bias_row)


def conv_weight_kernel(first_ref, second_ref, one_ref, two_ref, spread):
    odd = lax.axis_index("depth") % 2
    lane = lanes_of((1, 128))

    def arrange(source, start, count, out_ref):
        for pair in range(count // 2):
            chunk = source[:, pl.ds(start + pair * 128, 128)].astype(F32)
            spread[pl.ds(2 * pair, 27, stride=STEP), :] = chunk
            spread[pl.ds(2 * pair + 1, 27, stride=STEP), :] = pltpu.roll(chunk, 64, 1)
        for eh in range(3):
            for ew in range(3):
                for zp in range(2):
                    for zo in range(2):
                        halves = []
                        for zi in range(2):
                            ed = 2 * zp + zi - zo
                            if 0 <= ed < 3:
                                ed = ed + odd * (2 - 2 * ed)
                                start_row = pl.multiple_of((9 * ed + 3 * eh + ew) * STEP, 8)
                                tap = spread[pl.ds(start_row, count), :]
                                halves.append(pltpu.roll(tap, 64, 1) if zi else tap)
                            else:
                                halves.append(jnp.zeros((count, 128), F32))
                        block = jnp.where(lane < 64, halves[0], halves[1])
                        row, column = (ew * 2 + zo) * count, (eh * 2 + zp) * 128
                        out_ref[pl.ds(row, count), pl.ds(column, 128)] = block.astype(BF16)

    arrange(first_ref, 0, 64, one_ref)
    arrange(second_ref, pl.multiple_of(lax.axis_index("filt") * 2048, 2048), 32, two_ref)


def prepare_convs(first, second):
    return pl.pallas_call(
        conv_weight_kernel,
        out_shape=(jax.ShapeDtypeStruct((384, 768), BF16), jax.ShapeDtypeStruct((192, 768), BF16)),
        in_specs=[VMEM, VMEM],
        out_specs=(VMEM, VMEM),
        scratch_shapes=[pltpu.VMEM((32 * STEP, 128), F32)],
        compiler_params=params(12),
        cost_estimate=cost(10**9, 2 * 2**20),
        name="prepare_convs",
    )(first, second)


def has_chip_beside():
    depth = lax.axis_index("depth")
    outside = (depth == 0) | (depth == lax.axis_size("depth") - 1)
    return jnp.where(outside, 0.0, 1.0).astype(F32)


def place_plane(plane, ref):
    ref[0:64, :] = jnp.zeros((64, 128), BF16)
    ref[64:1088, :] = plane.T
    ref[1088:1152, :] = jnp.zeros((64, 128), BF16)


def upsample(low_ref, high_ref, weight_ref, bias, zz, a):
    start = a * 64
    lhs = jnp.concatenate(
        [ref[start + hk * 64 : start + hk * 64 + 1024, :] for hk in range(2) for ref in (low_ref, high_ref)], axis=1
    )
    total = lax.dot_general(lhs, weight_ref[a, zz], NT, preferred_element_type=F32)
    width = lax.broadcasted_iota(jnp.int32, (1024, 128), 0) % 64
    aside = total[:, 128:256]
    before = jnp.where(width == 0, 0.0, pltpu.roll(aside, 1, 0))
    after = jnp.where(width == 63, 0.0, pltpu.roll(aside, 1023, 0))
    low_lanes = lanes_of((1024, 128)) < 64
    pair = (before, after) if zz == 0 else (after, before)
    return total[:, 0:128] + jnp.where(low_lanes, *pair) + bias


def interleave(low, high, a, natural):
    low_lanes = lanes_of((1024, 128)) < 64
    even = jnp.where(low_lanes, low, high)
    uneven = pltpu.roll(jnp.where(low_lanes, high, low), 64, 1)
    for h in range(16):
        for b, value in ((0, even), (1, uneven)):
            natural[pl.ds((2 * h + a) * 128 + b, 64, stride=2), :] = value[h * 64 : h * 64 + 64]


def place_pair(natural, ref):
    ref[0:128, :] = jnp.zeros((128, 128), BF16)
    ref[128:4224, :] = natural[...].astype(BF16)
    ref[4224:4352, :] = jnp.zeros((128, 128), BF16)


def column_of(row):
    return jnp.broadcast_to(row, (128, 128)).T


def combine(taps, count, h):
    where = pl.ds(h * 128, 128)
    column = lanes_of((count, 128))
    value = taps[count : 2 * count, where]
    value = value + jnp.where(column == 0, 0.0, pltpu.roll(taps[0:count, where], 1, 1))
    return value + jnp.where(column == 127, 0.0, pltpu.roll(taps[2 * count : 3 * count, where], 127, 1))


def hide(pairs, weight_ref, bias_ref, taps, keep, ref):
    rhs = jnp.concatenate([pair[eh * 128 : eh * 128 + 4096, :] for eh in range(3) for pair in pairs], axis=1)
    taps[...] = lax.dot_general(weight_ref[...], rhs, NT, preferred_element_type=F32)
    row = bias_ref[...]
    bias = column_of(jnp.concatenate([row, row], axis=1))
    ref[:, 0:128] = jnp.zeros((128, 128), BF16)
    ref[:, 4224:4352] = jnp.zeros((128, 128), BF16)
    for h in range(32):
        value = leaky(combine(taps, 128, h) + bias)
        if keep is not None:
            value = value * keep
        ref[:, (h + 1) * 128 : (h + 2) * 128] = value.astype(BF16)


def start_kernel(own_ref, near_ref, up_own_ref, up_near_ref, up_far_ref, up_weight, bias_ref, cells, kept):
    odd = lax.axis_index("depth") % 2
    filt = lax.axis_index("filt")

    for k in range(64):
        kd, kh, kw = 3 - k // 16, 3 - (k // 4) % 4, k % 4
        zin, zz = kd // 2, kd % 2
        hk, a = kh // 2, kh % 2
        place = ((3, 0, 1, 2), (2, 1, 0, 3))[zz][kw]
        half, rest = k // 32, k % 16
        source = pl.ds(pl.multiple_of(((k // 16 % 2 + odd) % 2 * 16 + rest) * 32, 32), 32)
        column = pl.ds((hk * 2 + zin) * 128, 128)
        mine = up_own_ref[(half + odd) % 2, source, :]
        up_weight[a, zz, pl.ds(pl.multiple_of(64 * place + 32 * filt, 32), 32), column] = mine
        theirs = (up_near_ref, up_far_ref)[half][source, :]
        up_weight[a, zz, pl.ds(pl.multiple_of(64 * place + 32 - 32 * filt, 32), 32), column] = theirs

    def bias_of(block):
        parts = block.astype(F32)
        return parts[0:1] + parts[1:2] + parts[2:3]

    mine = bias_of(up_own_ref[0, pl.ds(1024, 16), :])
    theirs = bias_of(up_near_ref[pl.ds(1024, 16), :])
    is_mine = (lanes_of((1, 128)) // 32) % 2 == filt
    bias = jnp.where(is_mine, mine, theirs)
    bias_ref[...] = jnp.broadcast_to(bias, (8, 128))

    place_plane(own_ref[...], cells.at[0])
    place_plane(near_ref[...], cells.at[1])
    for zz in range(2):
        for a in range(2):
            kept[zz, a] = upsample(cells.at[0], cells.at[1], up_weight, bias, zz, a).astype(BF16)


def middle_kernel(next_ref, cells, kept, up_weight, bias_ref, near, pair_ref, low_kept, natural):
    place_plane(next_ref[...], near)
    bias = bias_ref[0:1]
    for a in range(2):
        low_kept[a] = upsample(near, cells.at[0], up_weight, bias, 1, a).astype(BF16)
        low = upsample(near, cells.at[0], up_weight, bias, 0, a)
        interleave(low, kept[1, a].astype(F32), a, natural)
    place_pair(natural, pair_ref)


def late_kernel(
    last_ref, cells, kept, up_weight, bias_ref, pair_ref, one_ref, bias_one_ref,
    hidden,
    edge, second, natural, taps,
):
    place_plane(last_ref[...], edge)
    bias = bias_ref[0:1]
    for a in range(2):
        high = upsample(cells.at[1], edge, up_weight, bias, 1, a)
        interleave(kept[0, a].astype(F32), high, a, natural)
    place_pair(natural, second)
    hide((pair_ref, second), one_ref, bias_one_ref, taps, None, hidden)


def end_kernel(
    after_ref, near, low_kept, up_weight, bias_ref, pair_ref, hidden_ref, one_ref, two_ref, bias_one_ref, bias_two_ref,
    out_ref,
    edge, first, natural, taps, hidden, rows_out,
):
    odd = lax.axis_index("depth") % 2
    keep = has_chip_beside()
    place_plane(after_ref[...], edge)
    bias = bias_ref[0:1]
    for a in range(2):
        low = upsample(edge, near, up_weight, bias, 0, a) * keep
        interleave(low, low_kept[a].astype(F32) * keep, a, natural)
    place_pair(natural, first)
    upper = lax.broadcasted_iota(jnp.int32, (128, 128), 0) < 64
    hide((first, pair_ref), one_ref, bias_one_ref, taps, jnp.where(upper, keep, 1.0), hidden)

    rhs = jnp.concatenate(
        [ref[:, eh * 128 : eh * 128 + 4096] for eh in range(3) for ref in (hidden, hidden_ref)], axis=0
    )
    taps[0:192, :] = jnp.dot(two_ref[...], rhs, preferred_element_type=F32)
    row = bias_two_ref[...]
    row = jnp.where(lax.axis_index("filt") == 0, row[:, 0:32], row[:, 32:64])
    bias = column_of(jnp.concatenate([row] * 4, axis=1))[0:64]
    for h in range(32):
        value = leaky(combine(taps, 64, h) + bias)
        for z in range(2):
            rows_out[pl.ds((z + odd) % 2 * 32 + h, 32, stride=STEP), :] = value[z * 32 : z * 32 + 32]
    out_ref[...] = rows_out[...].reshape(32, STEP, 128)[:, 0:64].reshape(32, 2, 32, 128).astype(BF16)


def start(*operands):
    return pl.pallas_call(
        start_kernel,
        out_shape=(
            jax.ShapeDtypeStruct((2, 2, 256, 512), BF16),
            jax.ShapeDtypeStruct((8, 128), F32),
            jax.ShapeDtypeStruct((2, 1152, 128), BF16),
            jax.ShapeDtypeStruct((2, 2, 1024, 128), BF16),
        ),
        in_specs=[VMEM] * 5,
        out_specs=(VMEM,) * 4,
        compiler_params=params(16),
        cost_estimate=cost(2 * 10**9, 4 * 2**20),
        name="start",
    )(*operands)


def middle(*operands):
    return pl.pallas_call(
        middle_kernel,
        out_shape=(
            jax.ShapeDtypeStruct((1152, 128), BF16),
            jax.ShapeDtypeStruct((4352, 128), BF16),
            jax.ShapeDtypeStruct((2, 1024, 128), BF16),
        ),
        in_specs=[VMEM] * 5,
        out_specs=(VMEM,) * 3,
        scratch_shapes=[pltpu.VMEM((4096, 128), F32)],
        compiler_params=params(16),
        cost_estimate=cost(2 * 10**9, 4 * 2**20),
        name="middle",
    )(*operands)


def late(*operands):
    return pl.pallas_call(
        late_kernel,
        out_shape=jax.ShapeDtypeStruct((128, 4352), BF16),
        in_specs=[VMEM] * 8,
        out_specs=VMEM,
        scratch_shapes=[
            pltpu.VMEM((1152, 128), BF16),
            pltpu.VMEM((4352, 128), BF16),
            pltpu.VMEM((4096, 128), F32),
            pltpu.VMEM((384, 4096), F32),
        ],
        compiler_params=params(28),
        cost_estimate=cost(5 * 10**9, 4 * 2**20),
        name="late",
    )(*operands)


def end(*operands):
    return pl.pallas_call(
        end_kernel,
        out_shape=jax.ShapeDtypeStruct((32, 2, 32, 128), BF16),
        in_specs=[VMEM] * 11,
        out_specs=VMEM,
        scratch_shapes=[
            pltpu.VMEM((1152, 128), BF16),
            pltpu.VMEM((4352, 128), BF16),
            pltpu.VMEM((4096, 128), F32),
            pltpu.VMEM((384, 4096), F32),
            pltpu.VMEM((128, 4352), BF16),
            pltpu.VMEM((32 * STEP, 128), F32),
        ],
        compiler_params=params(28),
        cost_estimate=cost(5 * 10**9, 4 * 2**20),
        name="end",
    )(*operands)


def shards(volume, up_weight, up_bias, first_weight, first_bias, second_weight, second_bias):
    devices = lax.axis_size("depth")
    filt = lax.axis_index("filt")
    swap = [(0, 1), (1, 0)]
    siblings = [(i, i ^ 1) for i in range(devices)]
    across = [(i, i + 1) for i in range(1, devices - 1, 2)]
    across = across + [(j, i) for i, j in across]
    outward = [(i, i + 2 - i % 2 * 4) for i in range(devices) if 0 <= i + 2 - i % 2 * 4 < devices]

    mine = volume.reshape(64, 1024)
    theirs = lax.ppermute(mine, "filt", swap)
    up_own, up_send = prepare_up(up_weight, up_bias[None])
    up_near = lax.ppermute(up_send, "filt", swap)
    own = jnp.where(filt == 0, jnp.concatenate([mine, theirs]), jnp.concatenate([theirs, mine]))
    beyond = lax.ppermute(own, "depth", across)
    after = lax.ppermute(own, "depth", outward)
    near = lax.ppermute(own, "depth", siblings)
    up_far = lax.ppermute(up_near, "depth", siblings)
    last = lax.ppermute(beyond, "depth", siblings)
    one, two = prepare_convs(first_weight, second_weight)
    weight, bias, cells, kept = start(own, near, up_own, up_near, up_far)
    next_cells, pair, low_kept = middle(beyond, cells, kept, weight, bias)
    hidden = late(last, cells, kept, weight, bias, pair, one, first_bias[None])
    return end(after, next_cells, low_kept, weight, bias, pair, hidden, one, two, first_bias[None], second_bias[None])


def solution(mesh):
    placed = (P("filt", "depth", None), P(None, "filt"), P("filt"), P(), P(), P(), P())
    return jax.shard_map(
        shards,
        mesh=mesh,
        in_specs=placed,
        out_specs=P("filt", "depth", None, None),
        check_vma=False,
    )
```

```python
import jax
import jax.numpy as jnp
from jax import lax
from jax.experimental import pallas as pl
from jax.experimental.pallas import tpu as pltpu
from jax.sharding import PartitionSpec as P


F32 = jnp.float32
BF16 = jnp.bfloat16
STEP = 72
PART = 16
PART_STEP = 40
VMEM = pl.BlockSpec(memory_space=pltpu.VMEM)
SMEM = pl.BlockSpec(memory_space=pltpu.SMEM)
NT = (((1,), (1,)), ((), ()))


def params(mebibytes):
    return pltpu.CompilerParams(vmem_limit_bytes=mebibytes * 2**20)


def cost(flops, count):
    return pl.CostEstimate(flops=flops, bytes_accessed=count, transcendentals=0)


def lanes_of(shape):
    return lax.broadcasted_iota(jnp.int32, shape, len(shape) - 1)


def leaky(value):
    return jnp.maximum(value, 0.2 * value)


def up_weight_kernel(weight_ref, bias_ref, own_ref, send_ref, rows):
    turned = weight_ref[...].astype(F32).T
    for o in range(32):
        rows[o * STEP : o * STEP + 64, :] = turned[o * 64 : o * 64 + 64]
    for k in range(64):
        block = rows[pl.ds(k, 32, stride=STEP), :]
        own_ref[k // 32, pl.ds((k % 32) * 32, 32), :] = block.astype(BF16)
    bias = jnp.concatenate([bias_ref[...]] * 4, axis=1)
    high = bias.astype(BF16).astype(F32)
    middle = (bias - high).astype(BF16).astype(F32)
    low = bias - high - middle
    row = lax.broadcasted_iota(jnp.int32, (16, 128), 0)
    parts = jnp.where(row == 0, high, jnp.where(row == 1, middle, jnp.where(row == 2, low, 0.0)))
    for half in range(2):
        own_ref[half, pl.ds(1024, 16), :] = parts.astype(BF16)
    send_ref[...] = own_ref[lax.axis_index("depth") % 2]


def prepare_up(weight, bias_row):
    return pl.pallas_call(
        up_weight_kernel,
        out_shape=(jax.ShapeDtypeStruct((2, 1040, 128), BF16), jax.ShapeDtypeStruct((1040, 128), BF16)),
        in_specs=[VMEM, VMEM],
        out_specs=(VMEM, VMEM),
        scratch_shapes=[pltpu.VMEM((32 * STEP, 128), F32)],
        compiler_params=params(12),
        cost_estimate=cost(10**9, 2 * 2**20),
        name="prepare_up",
    )(weight, bias_row)


def conv_weight_kernel(first_ref, second_ref, one_ref, two_ref, spread):
    odd = lax.axis_index("depth") % 2
    lane = lanes_of((1, 128))

    def arrange(source, start, count, out_ref):
        for pair in range(count // 2):
            chunk = source[:, pl.ds(start + pair * 128, 128)].astype(F32)
            spread[pl.ds(2 * pair, 27, stride=STEP), :] = chunk
            spread[pl.ds(2 * pair + 1, 27, stride=STEP), :] = pltpu.roll(chunk, 64, 1)
        for eh in range(3):
            for ew in range(3):
                for zp in range(2):
                    for zo in range(2):
                        halves = []
                        for zi in range(2):
                            ed = 2 * zp + zi - zo
                            if 0 <= ed < 3:
                                ed = ed + odd * (2 - 2 * ed)
                                start_row = pl.multiple_of((9 * ed + 3 * eh + ew) * STEP, 8)
                                tap = spread[pl.ds(start_row, count), :]
                                halves.append(pltpu.roll(tap, 64, 1) if zi else tap)
                            else:
                                halves.append(jnp.zeros((count, 128), F32))
                        block = jnp.where(lane < 64, halves[0], halves[1])
                        row, column = (ew * 2 + zo) * count, (eh * 2 + zp) * 128
                        out_ref[pl.ds(row, count), pl.ds(column, 128)] = block.astype(BF16)

    arrange(first_ref, 0, 64, one_ref)
    arrange(second_ref, pl.multiple_of(lax.axis_index("filt") * 2048, 2048), 32, two_ref)


def prepare_convs(first, second):
    return pl.pallas_call(
        conv_weight_kernel,
        out_shape=(jax.ShapeDtypeStruct((384, 768), BF16), jax.ShapeDtypeStruct((192, 768), BF16)),
        in_specs=[VMEM, VMEM],
        out_specs=(VMEM, VMEM),
        scratch_shapes=[pltpu.VMEM((32 * STEP, 128), F32)],
        compiler_params=params(12),
        cost_estimate=cost(10**9, 2 * 2**20),
        name="prepare_convs",
    )(first, second)


def has_chip_beside():
    depth = lax.axis_index("depth")
    outside = (depth == 0) | (depth == lax.axis_size("depth") - 1)
    return jnp.where(outside, 0.0, 1.0).astype(F32)


def turn_kernel(mine_ref, theirs_ref, out_ref):
    is_low = lax.axis_index("filt") == 0
    mine, theirs = mine_ref[...], theirs_ref[...]
    out_ref[...] = jnp.concatenate([jnp.where(is_low, mine, theirs), jnp.where(is_low, theirs, mine)], axis=0).T


def turn(mine, theirs):
    return pl.pallas_call(
        turn_kernel,
        out_shape=jax.ShapeDtypeStruct((1024, 128), BF16),
        in_specs=[VMEM, VMEM],
        out_specs=VMEM,
        compiler_params=params(8),
        cost_estimate=cost(10**8, 2**19),
        name="turn",
    )(mine, theirs)


def place_plane(plane, ref):
    ref[0:64, :] = jnp.zeros((64, 128), BF16)
    ref[64:1088, :] = plane
    ref[1088:1152, :] = jnp.zeros((64, 128), BF16)


def upsample(low_ref, high_ref, weight_ref, bias, zz, a):
    start = a * 64
    lhs = jnp.concatenate(
        [ref[start + hk * 64 : start + hk * 64 + 1024, :] for hk in range(2) for ref in (low_ref, high_ref)], axis=1
    )
    total = lax.dot_general(lhs, weight_ref[a, zz], NT, preferred_element_type=F32)
    width = lax.broadcasted_iota(jnp.int32, (1024, 128), 0) % 64
    aside = total[:, 128:256]
    before = jnp.where(width == 0, 0.0, pltpu.roll(aside, 1, 0))
    after = jnp.where(width == 63, 0.0, pltpu.roll(aside, 1023, 0))
    low_lanes = lanes_of((1024, 128)) < 64
    pair = (before, after) if zz == 0 else (after, before)
    return total[:, 0:128] + jnp.where(low_lanes, *pair) + bias


def interleave(low, high, a, natural):
    low_lanes = lanes_of((1024, 128)) < 64
    even = jnp.where(low_lanes, low, high)
    uneven = pltpu.roll(jnp.where(low_lanes, high, low), 64, 1)
    for h in range(16):
        for b, value in ((0, even), (1, uneven)):
            natural[pl.ds((2 * h + a) * 128 + b, 64, stride=2), :] = value[h * 64 : h * 64 + 64]


def place_pair(natural, ref):
    ref[0:128, :] = jnp.zeros((128, 128), BF16)
    ref[128:4224, :] = natural[...].astype(BF16)
    ref[4224:4352, :] = jnp.zeros((128, 128), BF16)


def column_of(row):
    return jnp.broadcast_to(row, (128, 128)).T


def combine(taps, count, h):
    where = slice(h * 128, h * 128 + 128)
    column = lanes_of((count, 128))
    value = taps[count : 2 * count, where]
    value = value + jnp.where(column == 0, 0.0, pltpu.roll(taps[0:count, where], 1, 1))
    return value + jnp.where(column == 127, 0.0, pltpu.roll(taps[2 * count : 3 * count, where], 127, 1))


def hide(pairs, weight_ref, bias_ref, taps, keep, ref):
    rhs = jnp.concatenate([pair[eh * 128 : eh * 128 + 4096, :] for eh in range(3) for pair in pairs], axis=1)
    taps[...] = lax.dot_general(weight_ref[...], rhs, NT, preferred_element_type=F32)
    row = bias_ref[...]
    bias = column_of(jnp.concatenate([row, row], axis=1))
    ref[:, 0:128] = jnp.zeros((128, 128), BF16)
    ref[:, 4224:4352] = jnp.zeros((128, 128), BF16)
    for h in range(32):
        value = leaky(combine(taps, 128, h) + bias)
        if keep is not None:
            value = value * keep
        ref[:, (h + 1) * 128 : (h + 2) * 128] = value.astype(BF16)


def start_kernel(own_ref, near_ref, up_own_ref, up_near_ref, up_far_ref, up_weight, bias_ref, cells, kept):
    odd = lax.axis_index("depth") % 2
    filt = lax.axis_index("filt")

    for k in range(64):
        kd, kh, kw = 3 - k // 16, 3 - (k // 4) % 4, k % 4
        zin, zz = kd // 2, kd % 2
        hk, a = kh // 2, kh % 2
        place = ((3, 0, 1, 2), (2, 1, 0, 3))[zz][kw]
        half, rest = k // 32, k % 16
        source = pl.ds(pl.multiple_of(((k // 16 % 2 + odd) % 2 * 16 + rest) * 32, 32), 32)
        column = pl.ds((hk * 2 + zin) * 128, 128)
        mine = up_own_ref[(half + odd) % 2, source, :]
        up_weight[a, zz, pl.ds(pl.multiple_of(64 * place + 32 * filt, 32), 32), column] = mine
        theirs = (up_near_ref, up_far_ref)[half][source, :]
        up_weight[a, zz, pl.ds(pl.multiple_of(64 * place + 32 - 32 * filt, 32), 32), column] = theirs

    def bias_of(block):
        parts = block.astype(F32)
        return parts[0:1] + parts[1:2] + parts[2:3]

    mine = bias_of(up_own_ref[0, pl.ds(1024, 16), :])
    theirs = bias_of(up_near_ref[pl.ds(1024, 16), :])
    is_mine = (lanes_of((1, 128)) // 32) % 2 == filt
    bias = jnp.where(is_mine, mine, theirs)
    bias_ref[...] = jnp.broadcast_to(bias, (8, 128))

    place_plane(own_ref[...], cells.at[0])
    place_plane(near_ref[...], cells.at[1])
    for zz in range(2):
        for a in range(2):
            kept[zz, a] = upsample(cells.at[0], cells.at[1], up_weight, bias, zz, a).astype(BF16)


def middle_kernel(next_ref, cells, kept, up_weight, bias_ref, near, pair_ref, low_kept, natural):
    place_plane(next_ref[...], near)
    bias = bias_ref[0:1]
    for a in range(2):
        low_kept[a] = upsample(near, cells.at[0], up_weight, bias, 1, a).astype(BF16)
        low = upsample(near, cells.at[0], up_weight, bias, 0, a)
        interleave(low, kept[1, a].astype(F32), a, natural)
    place_pair(natural, pair_ref)


def late_kernel(
    last_ref, cells, kept, up_weight, bias_ref, pair_ref, one_ref, bias_one_ref,
    hidden,
    edge, second, natural, taps,
):
    place_plane(last_ref[...], edge)
    bias = bias_ref[0:1]
    for a in range(2):
        high = upsample(cells.at[1], edge, up_weight, bias, 1, a)
        interleave(kept[0, a].astype(F32), high, a, natural)
    place_pair(natural, second)
    hide((pair_ref, second), one_ref, bias_one_ref, taps, None, hidden)


def end_kernel(
    after_ref, near, low_kept, up_weight, bias_ref, pair_ref, hidden_ref, one_ref, two_ref, bias_one_ref, bias_two_ref,
    out_ref,
    edge, first, natural, taps, hidden, rows_out, decoded, sent,
):
    odd = lax.axis_index("depth") % 2
    keep = has_chip_beside()
    place_plane(after_ref[...], edge)
    bias = bias_ref[0:1]
    for a in range(2):
        low = upsample(edge, near, up_weight, bias, 0, a) * keep
        interleave(low, low_kept[a].astype(F32) * keep, a, natural)
    place_pair(natural, first)
    upper = lax.broadcasted_iota(jnp.int32, (128, 128), 0) < 64
    hide((first, pair_ref), one_ref, bias_one_ref, taps, jnp.where(upper, keep, 1.0), hidden)

    row = bias_two_ref[...]
    row = jnp.where(lax.axis_index("filt") == 0, row[:, 0:32], row[:, 32:64])
    bias = column_of(jnp.concatenate([row] * 4, axis=1))[0:64]
    copies = []
    for base in range(0, 32, PART):
        rhs = jnp.concatenate(
            [
                ref[:, (base + eh) * 128 : (base + eh + PART) * 128]
                for eh in range(3)
                for ref in (hidden, hidden_ref)
            ],
            axis=0,
        )
        part = base // PART
        total = jnp.dot(two_ref[...], rhs, preferred_element_type=F32)
        for h in range(PART):
            value = leaky(combine(total, 64, h) + bias)
            for z in range(2):
                rows_out[part, pl.ds((z + odd) % 2 * PART + h, 32, stride=PART_STEP), :] = value[z * 32 : z * 32 + 32]
        block = rows_out[part].reshape(32, PART_STEP, 128)[:, 0 : 2 * PART].reshape(32, 2, PART, 128)
        decoded[part] = block.astype(BF16)
        where = out_ref.at[:, :, base : base + PART, :]
        copies.append(pltpu.make_async_copy(decoded.at[part], where, sent.at[part]))
        copies[-1].start()
    for copy in copies:
        copy.wait()


def start(*operands):
    return pl.pallas_call(
        start_kernel,
        out_shape=(
            jax.ShapeDtypeStruct((2, 2, 256, 512), BF16),
            jax.ShapeDtypeStruct((8, 128), F32),
            jax.ShapeDtypeStruct((2, 1152, 128), BF16),
            jax.ShapeDtypeStruct((2, 2, 1024, 128), BF16),
        ),
        in_specs=[VMEM] * 5,
        out_specs=(VMEM,) * 4,
        compiler_params=pltpu.CompilerParams(vmem_limit_bytes=16 * 2**20),
        cost_estimate=cost(2 * 10**9, 4 * 2**20),
        name="start",
    )(*operands)


def middle(*operands):
    return pl.pallas_call(
        middle_kernel,
        out_shape=(
            jax.ShapeDtypeStruct((1152, 128), BF16),
            jax.ShapeDtypeStruct((4352, 128), BF16),
            jax.ShapeDtypeStruct((2, 1024, 128), BF16),
        ),
        in_specs=[VMEM] * 5,
        out_specs=(VMEM,) * 3,
        scratch_shapes=[pltpu.VMEM((4096, 128), F32)],
        compiler_params=params(16),
        cost_estimate=cost(2 * 10**9, 4 * 2**20),
        name="middle",
    )(*operands)


def late(*operands):
    return pl.pallas_call(
        late_kernel,
        out_shape=jax.ShapeDtypeStruct((128, 4352), BF16),
        in_specs=[VMEM] * 8,
        out_specs=VMEM,
        scratch_shapes=[
            pltpu.VMEM((1152, 128), BF16),
            pltpu.VMEM((4352, 128), BF16),
            pltpu.VMEM((4096, 128), F32),
            pltpu.VMEM((384, 4096), F32),
        ],
        compiler_params=params(28),
        cost_estimate=cost(5 * 10**9, 4 * 2**20),
        name="late",
    )(*operands)


def end(*operands):
    return pl.pallas_call(
        end_kernel,
        out_shape=jax.ShapeDtypeStruct((32, 2, 32, 128), BF16),
        in_specs=[VMEM] * 11,
        out_specs=pl.BlockSpec(memory_space=pl.ANY),
        scratch_shapes=[
            pltpu.VMEM((1152, 128), BF16),
            pltpu.VMEM((4352, 128), BF16),
            pltpu.VMEM((4096, 128), F32),
            pltpu.VMEM((384, 4096), F32),
            pltpu.VMEM((128, 4352), BF16),
            pltpu.VMEM((32 // PART, 32 * PART_STEP, 128), F32),
            pltpu.VMEM((32 // PART, 32, 2, PART, 128), BF16),
            pltpu.SemaphoreType.DMA((32 // PART,)),
        ],
        compiler_params=params(28),
        cost_estimate=cost(5 * 10**9, 4 * 2**20),
        name="end",
    )(*operands)


def shards(volume, up_weight, up_bias, first_weight, first_bias, second_weight, second_bias):
    devices = lax.axis_size("depth")
    swap = [(0, 1), (1, 0)]
    siblings = [(i, i ^ 1) for i in range(devices)]
    across = [(i, i + 1) for i in range(1, devices - 1, 2)]
    across = across + [(j, i) for i, j in across]
    outward = [(i, i + 2 - i % 2 * 4) for i in range(devices) if 0 <= i + 2 - i % 2 * 4 < devices]

    mine = volume.reshape(64, 1024)
    theirs = lax.ppermute(mine, "filt", swap)
    up_own, up_send = prepare_up(up_weight, up_bias[None])
    weights = [(2 * i + f, 2 * ((i + devices // 2) % devices) + 1 - f) for i in range(devices) for f in range(2)]
    up_near = lax.ppermute(up_send, ("depth", "filt"), weights)
    own = turn(mine, theirs)
    beyond = lax.ppermute(own, "depth", across)
    after = lax.ppermute(own, "depth", outward)
    near = lax.ppermute(own, "depth", siblings)
    up_far = lax.ppermute(up_near, "depth", siblings)
    last = lax.ppermute(beyond, "depth", siblings)
    one, two = prepare_convs(first_weight, second_weight)
    weight, bias, cells, kept = start(own, near, up_own, up_near, up_far)
    next_cells, pair, low_kept = middle(beyond, cells, kept, weight, bias)
    hidden = late(last, cells, kept, weight, bias, pair, one, first_bias[None])
    return end(after, next_cells, low_kept, weight, bias, pair, hidden, one, two, first_bias[None], second_bias[None])


def solution(mesh):
    placed = (P("filt", "depth", None), P(None, "filt"), P("filt"), P(), P(), P(), P())
    return jax.shard_map(
        shards,
        mesh=mesh,
        in_specs=placed,
        out_specs=P("filt", "depth", None, None),
        check_vma=False,
    )
```
